32 devices in a mesh: batch: 4 (over y, x), tm: 4 (over z), tensor: 2 (over core).
Axes of the slice: x: 2, y: 2, z: 4, core: 2. Of those that a mesh axis runs over, the one named last changes fastest.
Arguments:
- q_raw: bfloat16 [4, 1536, 3072], P('batch', 'tm', 'tensor'), may hold values from -2500 to 2500
- k_raw: bfloat16 [4, 1536, 3072], P('batch', 'tm', 'tensor'), may hold values from -2500 to 2500
- values: bfloat16 [4, 1536, 3072], P('batch', 'tm', 'tensor'), may hold values from -6 to 6
- grad_out: bfloat16 [4, 1536, 3072], P('batch', 'tm', 'tensor'), may hold values from -16 to 16
- gain_q: float32 [3072], P('tensor'), may hold values from 0.25 to 1.75
- gain_k: float32 [3072], P('tensor'), may hold values from 0.25 to 1.75
- tile_lists: int32 [4, 4, 3], P('batch', 'tm'), may hold values from -1 to 3, as said below
Outputs:
- grad_q: bfloat16 [4, 1536, 3072], P('batch', 'tm', 'tensor')
- grad_k: bfloat16 [4, 1536, 3072], P('batch', 'tm', 'tensor')
- grad_values: bfloat16 [4, 1536, 3072], P('batch', 'tm', 'tensor')
- grad_gain_q: float32 [3072], P('tensor')
- grad_gain_k: float32 [3072], P('tensor')
The draws below stay inside these ranges and needn't reach their ends.
Inputs may be any that keep to these rules, and one draw needn't show every extreme that they name: `tile_lists`: every entry is a key tile or -1 for an empty slot. A list names no tile twice, always names its own query tile, and names only tiles whose time slab (tile) differs from the query tile's by at most one; in every clip some list fills all 3 slots.
All inputs are finite; a program needn't handle non-finite values.
Results may differ from the reference program's by a relative error of at most 0.0107.
The reference program's roundings to bfloat16 on the way count: a program that leaves them out, or rounds other values in their place, can miss the bound.
Values may be sent and summed in bfloat16 or wider, within the bound.
A program may use at most 128 MiB of HBM per device.

```python
import math
from functools import partial
import jax
import jax.numpy as jnp
from jax import lax

HEADS = 24
HD = 128
SPT = 1
CLIPS = 4
QT = 4
TOKENS = 1536
WIDTH = 3072
KMAX = 3


def raw_pair(key):
    full_shape = (CLIPS, TOKENS, WIDTH)
    subkeys = jax.random.split(jax.random.fold_in(key, 11), 12)
    head_ids = jnp.arange(WIDTH) // HD
    rising = 1.0 + 2.0 * head_ids.astype(jnp.float32) / max(HEADS - 1, 1)
    head_top = math.log(10.0)
    results = []
    for member in range(2):
        offset = 4 * member
        base_noise = jnp.clip(jax.random.normal(subkeys[offset], full_shape, jnp.float32), -4.0, 4.0)
        row_scale = jnp.exp(jax.random.uniform(subkeys[offset + 1], (CLIPS, TOKENS, 1), jnp.float32, 0.0, math.log(10.0)))
        head_scale = jnp.exp(jax.random.uniform(subkeys[offset + 2], (CLIPS, 1, HEADS), jnp.float32, 0.0, head_top))
        head_cols = jnp.repeat(head_scale, HD, axis=2)
        jitter = jnp.exp(jax.random.uniform(subkeys[offset + 3], (CLIPS, 1, WIDTH), jnp.float32, math.log(0.5), math.log(2.0)))
        results.append(base_noise * row_scale * head_cols * jitter * rising[None, None, :])
    query_part, key_part = (results[0], results[1])
    return (query_part, key_part)


def draw_q_raw(key, part):
    query_part, key_part = raw_pair(key)
    return query_part.astype(jnp.bfloat16)


def draw_k_raw(key, part):
    query_part, key_part = raw_pair(key)
    return key_part.astype(jnp.bfloat16)


def draw_grad_out(key, part):
    subkeys = jax.random.split(jax.random.fold_in(key, 17), 1)
    ordinal = (jnp.arange(CLIPS)[:, None] * TOKENS + jnp.arange(TOKENS)[None, :]).astype(jnp.float32)
    rise_factor = 1.0 + 2.0 * ordinal / (CLIPS * TOKENS - 1)
    base_noise = jnp.clip(jax.random.normal(subkeys[0], (CLIPS, TOKENS, WIDTH), jnp.float32), -4.0, 4.0)
    return (base_noise * rise_factor[:, :, None]).astype(jnp.bfloat16)


def draw_tile_lists(key, part):
    subkeys = jax.random.split(jax.random.fold_in(key, 29), 3)
    spread = min(SPT, 3)
    slab_count = QT // SPT
    query_ids = jnp.arange(QT)
    query_slab = query_ids // SPT
    query_spot = query_ids % SPT
    candidate = jnp.arange(KMAX)
    time_step = candidate // spread - 1
    spot_step = candidate % spread
    window_start = jnp.clip(query_spot - 1, 0, SPT - spread)
    key_slab = query_slab[:, None] + time_step[None, :]
    key_spot = window_start[:, None] + spot_step[None, :]
    tile_ids = key_slab * SPT + key_spot
    exists = (key_slab >= 0) & (key_slab < slab_count)
    itself = (time_step[None, :] == 0) & (key_spot == query_spot[:, None])
    kept_slot = jax.random.randint(subkeys[0], (CLIPS, QT, KMAX), 0, 2) == 1
    full_row = jax.random.randint(subkeys[1], (CLIPS,), SPT, QT - SPT)
    forced = query_ids[None, :, None] == full_row[:, None, None]
    live_entry = exists[None] & (itself[None] | kept_slot | forced)
    entries = jnp.where(live_entry, tile_ids[None], -1)
    ranking = jnp.argsort(jax.random.randint(subkeys[2], (CLIPS, QT, KMAX), 0, 1 << 20) * KMAX + candidate[None, None, :], axis=-1)
    return jnp.take_along_axis(entries, ranking, axis=-1).astype(jnp.int32)


def shard_levels(key, extent, cuts, smallest, high):
    loudness, own = 1.0, jax.random.fold_in(key, 6)
    for dim, blocks in cuts:
        heights = jnp.exp(jax.random.uniform(jax.random.fold_in(own, dim), (blocks,), jnp.float32, smallest / len(cuts), high / len(cuts)))
        loudness = loudness * jnp.repeat(heights, extent[dim] // blocks).reshape([-1 if axis == dim else 1 for axis in range(len(extent))])
    return loudness


def centred(own_key, shape, scale, most, pieces=(), held_as=jnp.bfloat16):
    level = shard_levels(own_key, shape, pieces, -0.22, 0.18) if pieces else 1.0
    drawn = jax.random.normal(own_key, shape, jnp.float32) * scale * level
    return jnp.minimum(jnp.maximum(drawn, -most), most).astype(held_as)


def setup_inputs(seed: int = 0) -> dict:
    arg_keys = jax.random.split(jax.random.key(seed), 8)
    return {
        "q_raw": draw_q_raw(jax.random.fold_in(arg_keys[7], 71), 0),
        "k_raw": draw_k_raw(jax.random.fold_in(arg_keys[7], 71), 0),
        "values": centred(arg_keys[2], (CLIPS, TOKENS, WIDTH), 1.0, 6.0, ((0, 4), (1, 4), (2, 2))),
        "grad_out": draw_grad_out(jax.random.fold_in(arg_keys[7], 71), 0),
        "gain_q": jnp.clip(1.0 + 0.15 * jax.random.normal(arg_keys[4], (WIDTH,), jnp.float32), 0.25, 1.75),
        "gain_k": jnp.clip(1.0 + 0.15 * jax.random.normal(arg_keys[5], (WIDTH,), jnp.float32), 0.25, 1.75),
        "tile_lists": draw_tile_lists(jax.random.fold_in(arg_keys[7], 71), 0),
    }


EPSILON = 1e-06
MASKED_SCORE = -1e+30

def normalize_rows(raw_rows, gain_row):
    wide_rows = raw_rows.astype(jnp.float32)
    inverse = lax.rsqrt(lax.optimization_barrier(jnp.mean(wide_rows * wide_rows, axis=1)) + EPSILON)
    normed = (wide_rows * inverse[:, None] * gain_row[None, :]).astype(jnp.bfloat16)
    return (wide_rows, inverse, normed)

def undo_norm(wide_rows, inverse, gain_row, grad_normed):
    feature_count = wide_rows.shape[1]
    projection = lax.optimization_barrier(jnp.sum(wide_rows * gain_row[None, :] * grad_normed, axis=1))
    cubed = inverse * inverse * inverse
    grad_rows = inverse[:, None] * gain_row[None, :] * grad_normed - wide_rows * (cubed * projection / feature_count)[:, None]
    gain_term = lax.optimization_barrier(jnp.sum(grad_normed * wide_rows * inverse[:, None], axis=0))
    return (grad_rows.astype(jnp.bfloat16), gain_term)

def clip_pass(gain_q, gain_k, packed):
    query_raw, key_raw, value_rows, grad_rows, tile_rows = packed
    token_count, feature_count = query_raw.shape
    tile_count, slot_count = tile_rows.shape
    tile_len = token_count // tile_count
    head_count = feature_count // HD
    score_scale = HD ** (-0.5)
    query_wide, inverse_q, query_norm = normalize_rows(query_raw, gain_q)
    key_wide, inverse_k, key_norm = normalize_rows(key_raw, gain_k)
    tile_shape = (tile_count, tile_len, head_count, HD)
    query_tiles = lax.optimization_barrier(query_norm).astype(jnp.float32).reshape(tile_shape)
    key_tiles = lax.optimization_barrier(key_norm).astype(jnp.float32).reshape(tile_shape)
    value_tiles = value_rows.astype(jnp.float32).reshape(tile_shape)
    grad_tiles = grad_rows.astype(jnp.float32).reshape(tile_shape)

    def step(carry, number):
        key_sum, value_sum = carry
        entries = tile_rows[number]
        live_slots = entries >= 0
        safe_slots = jnp.clip(entries, 0, tile_count - 1)
        key_rows = key_tiles[safe_slots].reshape(slot_count * tile_len, head_count, HD)
        val_rows = value_tiles[safe_slots].reshape(slot_count * tile_len, head_count, HD)
        query_rows = query_tiles[number]
        grad_here = grad_tiles[number]
        scores = jnp.einsum('qhd,khd->hqk', query_rows, key_rows) * score_scale
        live_cols = jnp.repeat(live_slots, tile_len)
        scores = jnp.where(live_cols[None, None, :], scores, MASKED_SCORE)
        highest = lax.optimization_barrier(jnp.max(scores, axis=2, keepdims=True))
        exponent = jnp.exp(scores - highest)
        attn_probs = exponent / lax.optimization_barrier(jnp.sum(exponent, axis=2, keepdims=True))
        dprobs = jnp.einsum('qhd,khd->hqk', grad_here, val_rows)
        row_delta = lax.optimization_barrier(jnp.sum(attn_probs * dprobs, axis=2, keepdims=True))
        dscore = lax.optimization_barrier((attn_probs * (dprobs - row_delta)).astype(jnp.bfloat16)).astype(jnp.float32)
        probs_b = lax.optimization_barrier(attn_probs.astype(jnp.bfloat16)).astype(jnp.float32)
        grad_query = jnp.einsum('hqk,khd->qhd', dscore, key_rows) * score_scale
        grad_key = (jnp.einsum('hqk,qhd->khd', dscore, query_rows) * score_scale).reshape(slot_count, tile_len, head_count, HD)
        grad_value = jnp.einsum('hqk,qhd->khd', probs_b, grad_here).reshape(slot_count, tile_len, head_count, HD)
        return ((key_sum.at[safe_slots].add(grad_key), value_sum.at[safe_slots].add(grad_value)), grad_query)
    zero_tiles = jnp.zeros(tile_shape, jnp.float32)
    (key_sum, value_sum), query_grads = lax.scan(step, (zero_tiles, zero_tiles), jnp.arange(tile_count))
    grad_qn = query_grads.reshape(token_count, feature_count)
    grad_kn = key_sum.reshape(token_count, feature_count)
    grad_values = value_sum.reshape(token_count, feature_count).astype(jnp.bfloat16)
    grad_q, terms_q = undo_norm(query_wide, inverse_q, gain_q, grad_qn)
    grad_k, terms_k = undo_norm(key_wide, inverse_k, gain_k, grad_kn)
    return (grad_q, grad_k, grad_values, terms_q, terms_k)

def reference(q_raw, k_raw, values, grad_out, gain_q, gain_k, tile_lists):
    grad_q, grad_k, grad_values, terms_q, terms_k = lax.map(partial(clip_pass, gain_q, gain_k), (q_raw, k_raw, values, grad_out, tile_lists))
    factor_all = 1.0 / math.sqrt(CLIPS * TOKENS)
    return (grad_q, grad_k, grad_values, lax.optimization_barrier(jnp.sum(terms_q, axis=0)) * factor_all, lax.optimization_barrier(jnp.sum(terms_k, axis=0)) * factor_all)
```

```python
import math

import jax
import jax.numpy as jnp
from jax import lax
from jax.experimental import pallas as pl
from jax.experimental.pallas import tpu as pltpu
from jax.sharding import PartitionSpec as P

HD = 128
EPSILON = 1e-06
DEAD = 1e30
SCALE = HD ** (-0.5)
SCALE2 = SCALE * math.log2(math.e)
AHEAD = 2
FIRST = 3
PACE = 2
EXTRA = 3
MESH = pl.DeviceIdType.MESH


def cols_dot(left, right):
    return lax.dot_general(
        left, right, (((1,), (1,)), ((), ())), preferred_element_type=jnp.float32
    )


def rows_dot(left, right):
    return lax.dot_general(
        left, right, (((0,), (0,)), ((), ())), preferred_element_type=jnp.float32
    )


def tile_stats(key, value, query, grad):
    scores = cols_dot(key, query) * SCALE2
    highest = jnp.max(scores, axis=0, keepdims=True)
    exponent = jnp.exp2(scores - highest)
    dprobs = cols_dot(value, grad)
    total = jnp.sum(exponent, axis=0, keepdims=True)
    weighted = jnp.sum(exponent * dprobs, axis=0, keepdims=True)
    return highest + jnp.log2(total), weighted / total


def paced(step, heads, ahead):
    return PACE * (step - (heads - ahead)), step - 2


def attention_body(heads, list_hbm, q_hbm, k_hbm, v_hbm, g_hbm, gq_hbm, gk_hbm,
                   gq, gk, dv, sum_q, sum_k,
                   entries, gain_q, gain_k, q_raw, k_raw, v, g, q, k, dq, dk, inv, pull, squares, proj,
                   rq, rg, dq_out, dq_in, st_own, st_out, st_in, co_own, co_out, co_in,
                   pj_own, pj_out, pj_in, pq, terms, term_in, planes,
                   in_sem, sq_send, sq_recv, pk_send, pk_recv, pq_send, pq_recv,
                   tb_send, tb_recv, tz_send, tz_recv, pj_send, pj_recv,
                   bulk_send, bulk_recv, st_send, st_recv, co_send, co_recv, dq_send, dq_recv,
                   relay):
    rows, width = q.shape
    ahead = min(AHEAD, heads)
    first = min(FIRST, heads)
    core = lax.axis_index("tensor")
    cores = lax.axis_size("tensor")
    me = lax.axis_index("tm")
    peers = lax.axis_size("tm")
    clip = lax.axis_index("batch")
    clips = lax.axis_size("batch")
    levels = clips.bit_length() - 1
    assert clips == 1 << levels
    partners = [
        clip + (1 << level) * (1 - 2 * (lax.div(clip, 1 << level) % 2)) for level in range(levels)
    ]
    has = (me > 0, me < peers - 1)
    target = (jnp.maximum(me - 1, 0), jnp.minimum(me + 1, peers - 1))

    def column(head):
        return pl.ds(pl.multiple_of(head * HD, HD), HD)

    def remote(source, sink, send, recv, **where):
        return pltpu.make_async_remote_copy(
            src_ref=source, dst_ref=sink, send_sem=send, recv_sem=recv,
            device_id=where, device_id_type=MESH,
        )

    def grad_copy(head, side, slot):
        col = column(head)
        return remote(g_hbm.at[:, col], rg.at[slot, :, col],
                      bulk_send.at[side, 0, head], bulk_recv.at[slot, 0, head], tm=target[side])

    def query_copy(head, side, slot):
        col = column(head)
        return remote(q.at[:, col], rq.at[slot, :, col],
                      bulk_send.at[side, 1, head], bulk_recv.at[slot, 1, head], tm=target[side])

    def stat_copy(head, side, slot):
        return remote(st_out.at[side, head], st_in.at[slot, head],
                      st_send.at[side, head], st_recv.at[slot, head], tm=target[side])

    def comb_copy(head, side, slot):
        return remote(co_out.at[side, head], co_in.at[slot, head],
                      co_send.at[side, head], co_recv.at[slot, head], tm=target[side])

    def dq_copy(head, side, slot):
        col = column(head)
        return remote(dq_out.at[side, :, col], dq_in.at[slot, :, col],
                      dq_send.at[side, head], dq_recv.at[slot, head], tm=target[side])

    def pj_copy(side, slot):
        return remote(pj_out.at[side], pj_in.at[slot], pj_send.at[side], pj_recv.at[slot],
                      tm=target[side])

    def square_copy(index, slot, peer):
        return remote(squares.at[slot, index], squares.at[slot, index],
                      sq_send.at[index, peer], sq_recv.at[index, slot], tensor=peer)

    def proj_copy(slot, peer):
        return remote(proj.at[slot], proj.at[slot], pk_send.at[peer], pk_recv.at[slot], tensor=peer)

    def pq_copy(slot, peer):
        return remote(pq.at[slot], pq.at[slot], pq_send.at[peer], pq_recv.at[slot], tensor=peer)

    def term_copy(level):
        return remote(terms.at[level], term_in.at[level], tb_send.at[level], tb_recv.at[level],
                      batch=partners[level])

    def plane_copy(slot, peer):
        return remote(planes.at[slot], planes.at[slot], tz_send.at[peer], tz_recv.at[slot], tm=peer)

    def other(mine, count, i):
        return lax.rem(mine + i, count)

    def each_side(do):
        for side in range(2):
            @pl.when(has[side])
            def _():
                do(side)

    loads = [
        pltpu.make_async_copy(source, sink, in_sem.at[i])
        for i, (source, sink) in enumerate((
            (q_hbm, q_raw), (k_hbm, k_raw), (gq_hbm, gain_q), (gk_hbm, gain_k),
            (v_hbm, v), (g_hbm, g), (list_hbm, entries)))
    ]

    barrier = pltpu.get_barrier_semaphore()
    each_side(lambda side: pl.semaphore_signal(
        barrier, inc=1, device_id={"tm": target[side]}, device_id_type=MESH))
    for i in range(1, cores):
        pl.semaphore_signal(
            barrier, inc=1, device_id={"tensor": other(core, cores, i)}, device_id_type=MESH)
    for partner in partners:
        pl.semaphore_signal(barrier, inc=1, device_id={"batch": partner}, device_id_type=MESH)
    for load in loads:
        load.start()
    pl.semaphore_wait(
        barrier, has[0].astype(jnp.int32) + has[1].astype(jnp.int32) + cores - 1 + len(partners))

    for head in range(first):
        each_side(lambda side: grad_copy(head, side, 1 - side).start())

    block = math.gcd(rows, 128)
    for index, raw in enumerate((q_raw, k_raw)):
        loads[index].wait()
        for top in range(0, rows, block):
            total = jnp.zeros((block, HD), jnp.float32)
            for left in range(0, width, HD):
                wide = raw[top:top + block, left:left + HD].astype(jnp.float32)
                total = total + wide * wide
            squares[core, index, top:top + block, :] = total
        for i in range(1, cores):
            square_copy(index, core, other(core, cores, i)).start()

    for load in loads[2:4]:
        load.wait()
    for index, (raw, gain, out) in enumerate(((q_raw, gain_q, q), (k_raw, gain_k, k))):
        for i in range(1, cores):
            peer = other(core, cores, i)
            square_copy(index, core, peer).wait_send()
            square_copy(index, peer, peer).wait_recv()
        for top in range(0, rows, block):
            total = squares[0, index, top:top + block, :]
            for slot in range(1, cores):
                total = total + squares[slot, index, top:top + block, :]
            mean = jnp.sum(total, axis=1, keepdims=True) / (width * cores)
            inv[index, top:top + block, :] = jnp.broadcast_to(
                lax.rsqrt(mean + EPSILON), (block, HD))

        def norm(head, carry):
            col = column(head)
            out[:, col] = (
                raw[:, col].astype(jnp.float32) * inv[index] * gain[pl.ds(head, 1), :]
            ).astype(out.dtype)
            if index == 0:
                @pl.when(head < ahead)
                def _():
                    each_side(lambda side: query_copy(head, side, 1 - side).start())
            return carry

        lax.fori_loop(0, heads, norm, 0)

    for load in loads[4:]:
        load.wait()
    alive = tuple(
        has[side] & (
            (entries[0] == target[side]) | (entries[1] == target[side])
            | (entries[2] == target[side]))
        for side in range(2)
    )
    for side in range(2):
        @pl.when(jnp.logical_not(has[side]))
        def _():
            for ref in (rq, rg, dq_in, st_in, co_in, pj_in):
                ref[side] = jnp.zeros(ref.shape[1:], ref.dtype)
    pj_own[...] = jnp.zeros(pj_own.shape, jnp.float32)
    pj_out[...] = jnp.zeros(pj_out.shape, jnp.float32)
    proj[core] = jnp.zeros((rows, HD), jnp.float32)

    def put(ref, index, values):
        for row, value in enumerate(values):
            ref[index + (slice(row, row + 1), slice(None))] = value

    def combine(head):
        own = st_own[head, 0:1, :]
        sides = [st_in[side, head, 0:1, :] for side in range(2)]
        highest = own
        for side in range(2):
            highest = jnp.where(alive[side], jnp.maximum(highest, sides[side]), highest)
        weight = jnp.exp2(own - highest)
        total = weight
        delta = weight * st_own[head, 1:2, :]
        for side in range(2):
            weight = jnp.where(
                alive[side], jnp.exp2(jnp.minimum(sides[side] - highest, 0.0)), 0.0)
            total = total + weight
            delta = delta + jnp.where(alive[side], weight * st_in[side, head, 1:2, :], 0.0)
        whole = highest + jnp.log2(total)
        delta = delta / total
        put(co_own, (head,), (whole, delta))
        for side in range(2):
            put(co_out, (side, head), (jnp.where(alive[side], whole, DEAD), delta))

    def backward(head):
        col = column(head)
        key = k[:, col]
        value = v[:, col]
        key_total = None
        value_total = None
        for t in range(3):
            if t < 2:
                query, grad, stat = rq[t, :, col], rg[t, :, col], co_in.at[t]
            else:
                query, grad, stat = q[:, col], g[:, col], co_own
            scores = cols_dot(key, query) * SCALE2
            probs = jnp.exp2(scores - stat[head, 0:1, :])
            dprobs = cols_dot(value, grad)
            wide = probs * (dprobs - stat[head, 1:2, :])
            pulled = jnp.sum(wide * scores, axis=0, keepdims=True)
            dscore = wide.astype(jnp.bfloat16)
            probs_b = probs.astype(jnp.bfloat16)
            value_term = jnp.dot(probs_b, grad, preferred_element_type=jnp.float32)
            key_term = jnp.dot(dscore, query, preferred_element_type=jnp.float32)
            value_total = value_term if t == 0 else value_total + value_term
            key_total = key_term if t == 0 else key_total + key_term
            result = rows_dot(key, dscore).T * SCALE
            if t < 2:
                dq_out[t, :, col] = result.astype(dq_out.dtype)
                pj_out[t] = pj_out[t] + pulled
            else:
                dq[:, col] = result
                pj_own[...] = pj_own[...] + pulled
        key_total = key_total * SCALE
        dk[:, col] = key_total
        both = k_raw[:, col].astype(jnp.float32) * key_total
        terms[0, pl.ds(head, 1), :] = jnp.sum(both * inv[1], axis=0, keepdims=True)
        proj[core] = proj[core] + both * gain_k[pl.ds(head, 1), :]
        dv[:, col] = value_total.astype(dv.dtype)

    def start_dq(head, carry):
        each_side(lambda side: dq_copy(head, side, 1 - side).start())
        return carry

    def settle(head):
        def done(side):
            grad_copy(head, side, 1 - side).wait_send()
            query_copy(head, side, 1 - side).wait_send()
            stat_copy(head, side, 1 - side).wait_send()
            comb_copy(head, side, 1 - side).wait_send()

        each_side(done)

    rounds = peers - 2
    steps = heads + 2

    def relay_signal():
        each_side(lambda side: pl.semaphore_signal(
            relay.at[1 - side], inc=1, device_id={"tm": target[side]}, device_id_type=MESH))

    def relay_wait():
        each_side(lambda side: pl.semaphore_wait(relay.at[side], 1))

    def sent(s):
        wish, done = paced(s, heads, ahead)
        return jnp.maximum(jnp.minimum(wish, done), 0)

    def step(s, carry):
        @pl.when((s >= 1) & (s <= rounds))
        def _():
            relay_wait()

        @pl.when(s < rounds)
        def _():
            relay_signal()

        @pl.when(s < heads)
        def _():
            def arrive(side):
                grad_copy(s, side, side).wait_recv()
                query_copy(s, side, side).wait_recv()

            each_side(arrive)
            col = column(s)
            for side in range(2):
                put(st_out, (side, s), tile_stats(
                    k[:, col], v[:, col], rq[side, :, col], rg[side, :, col]))
            each_side(lambda side: stat_copy(s, side, 1 - side).start())

        @pl.when((s >= 1) & (s <= heads))
        def _():
            each_side(lambda side: stat_copy(s - 1, side, side).wait_recv())
            combine(s - 1)
            each_side(lambda side: comb_copy(s - 1, side, 1 - side).start())

        @pl.when(s + ahead < heads)
        def _():
            each_side(lambda side: query_copy(s + ahead, side, 1 - side).start())

        @pl.when(s + first < heads)
        def _():
            each_side(lambda side: grad_copy(s + first, side, 1 - side).start())

        lax.fori_loop(sent(s), sent(s + 1), start_dq, 0)

        @pl.when(s < heads)
        def _():
            col = column(s)
            put(st_own, (s,), tile_stats(k[:, col], v[:, col], q[:, col], g[:, col]))

        @pl.when(s >= 2)
        def _():
            each_side(lambda side: comb_copy(s - 2, side, side).wait_recv())
            backward(s - 2)

        @pl.when(s >= 3)
        def _():
            settle(s - 3)

        return carry

    lax.fori_loop(0, steps, step, 0)

    each_side(lambda side: pj_copy(side, 1 - side).start())
    if levels:
        term_copy(0).start()
    for i in range(1, cores):
        proj_copy(core, other(core, cores, i)).start()
    begun = max(min(*paced(steps, heads, ahead)), 0)
    early = min(begun + EXTRA, heads)
    lax.fori_loop(begun, early, start_dq, 0)

    if rounds >= steps:
        relay_wait()
        for _ in range(steps, rounds):
            relay_signal()
            relay_wait()

    def pull_of(index, projection):
        inverse = inv[index]
        pull[index] = inverse * inverse * projection / (width * cores)

    def finish(index, raw, gain, normed, out, head):
        col = column(head)
        out[:, col] = (
            inv[index] * gain[pl.ds(head, 1), :] * normed
            - raw[:, col].astype(jnp.float32) * pull[index]
        ).astype(out.dtype)

    for i in range(1, cores):
        peer = other(core, cores, i)
        proj_copy(core, peer).wait_send()
        proj_copy(peer, peer).wait_recv()
    total = proj[0]
    for slot in range(1, cores):
        total = total + proj[slot]
    pull_of(1, inv[1] * jnp.sum(total, axis=1, keepdims=True))

    each_side(lambda side: pj_copy(side, side).wait_recv())
    pq[core] = pj_own[...] + pj_in[0] + pj_in[1]
    for i in range(1, cores):
        pq_copy(core, other(core, cores, i)).start()

    for level in range(levels):
        term_copy(level).wait_send()
        term_copy(level).wait_recv()
        terms[level + 1] = terms[level] + term_in[level]
        if level + 1 < levels:
            term_copy(level + 1).start()
    planes[me] = terms[levels]
    for i in range(1, peers):
        plane_copy(me, other(me, peers, i)).start()
    lax.fori_loop(early, heads, start_dq, 0)

    def keys(head, carry):
        finish(1, k_raw, gain_k, dk[:, column(head)], gk, head)
        return carry

    lax.fori_loop(0, heads, keys, 0)

    for i in range(1, cores):
        peer = other(core, cores, i)
        pq_copy(core, peer).wait_send()
        pq_copy(peer, peer).wait_recv()
    row = pq[0]
    for slot in range(1, cores):
        row = row + pq[slot]
    pull_of(0, jnp.broadcast_to(row * (SCALE / SCALE2), (HD, rows)).T)

    settle(heads - 1)
    each_side(lambda side: pj_copy(side, 1 - side).wait_send())

    def queries(head, carry):
        @pl.when(head == heads - 1)
        def _():
            for i in range(1, peers):
                peer = other(me, peers, i)
                plane_copy(me, peer).wait_send()
                plane_copy(peer, peer).wait_recv()
            whole = jnp.sum(planes[...], axis=0) * (1.0 / math.sqrt(clips * peers * rows))
            sum_k[...] = whole
            sum_q[...] = whole * gain_k[...] / gain_q[...]

        @pl.when(head >= 1)
        def _():
            each_side(lambda side: dq_copy(head - 1, side, 1 - side).wait_send())

        each_side(lambda side: dq_copy(head, side, side).wait_recv())
        col = column(head)
        normed = (
            dq[:, col]
            + dq_in[0, :, col].astype(jnp.float32)
            + dq_in[1, :, col].astype(jnp.float32)
        )
        finish(0, q_raw, gain_q, normed, gq, head)
        return carry

    lax.fori_loop(0, heads, queries, 0)

    last = heads - 1
    each_side(lambda side: dq_copy(last, side, 1 - side).wait_send())


def attention(entries, query, key, value, grad, gain_q, gain_k):
    rows, width = query.shape
    heads = width // HD
    cores = lax.axis_size("tensor")
    peers = lax.axis_size("tm")
    clips = lax.axis_size("batch")
    vmem = pl.BlockSpec(memory_space=pltpu.VMEM)
    hbm = pl.BlockSpec(memory_space=pltpu.HBM)
    dma = pltpu.SemaphoreType.DMA
    full = jax.ShapeDtypeStruct((rows, width), jnp.bfloat16)
    gain = jax.ShapeDtypeStruct((heads, HD), jnp.float32)

    def f32(*shape):
        return pltpu.VMEM(shape, jnp.float32)

    def bf16(*shape):
        return pltpu.VMEM(shape, jnp.bfloat16)

    def body(*refs):
        attention_body(heads, *refs)

    pinned = [
        pltpu.with_memory_space_constraint(x, pltpu.HBM)
        for x in (entries, query, key, value, grad, gain_q, gain_k)
    ]
    return pl.pallas_call(
        body,
        out_shape=[full, full, full, gain, gain],
        in_specs=[hbm] * 7,
        out_specs=[vmem] * 5,
        scratch_shapes=(
            [pltpu.SMEM(entries.shape, jnp.int32)] + [f32(heads, HD)] * 2
            + [bf16(rows, width)] * 6 + [f32(rows, width)] * 2
            + [f32(2, rows, HD)] * 2 + [f32(cores, 2, rows, HD), f32(cores, rows, HD)]
            + [bf16(2, rows, width)] * 4
            + [f32(heads, 2, rows), f32(2, heads, 2, rows), f32(2, heads, 2, rows)] * 2
            + [f32(1, rows), f32(2, 1, rows), f32(2, 1, rows), f32(cores, 1, rows)]
            + [f32(clips.bit_length(), heads, HD)] * 2 + [f32(peers, heads, HD)]
            + [dma((7,)), dma((2, cores)), dma((2, cores))]
            + [dma((cores,))] * 4 + [dma((clips.bit_length(),))] * 2 + [dma((peers,))] * 2 + [dma((2,))] * 2
            + [dma((2, 2, heads))] * 2 + [dma((2, heads))] * 6
            + [pltpu.SemaphoreType.REGULAR((2,))]
        ),
        compiler_params=pltpu.CompilerParams(
            collective_id=0, has_side_effects=True, vmem_limit_bytes=36 << 20),
        name="attention",
    )(*pinned)


def hand_over(*arrays):
    count = len(arrays)
    hbm = pl.BlockSpec(memory_space=pltpu.HBM)

    def body(*refs):
        sems = refs[2 * count]
        copies = [
            pltpu.make_async_copy(refs[i], refs[count + i], sems.at[i]) for i in range(count)
        ]
        for copy in copies:
            copy.start()
        for copy in copies:
            copy.wait()

    return pl.pallas_call(
        body,
        out_shape=[jax.ShapeDtypeStruct(x.shape, x.dtype) for x in arrays],
        in_specs=[pl.BlockSpec(memory_space=pl.ANY)] * count,
        out_specs=[hbm] * count,
        scratch_shapes=[pltpu.SemaphoreType.DMA((count,))],
        compiler_params=pltpu.CompilerParams(vmem_limit_bytes=1 << 20),
        name="hand_over",
    )(*arrays)


def shards(q_raw, k_raw, values, grad_out, gain_q, gain_k, tile_lists):
    width = q_raw.shape[2]
    heads = width // HD
    grad_q, grad_k, grad_values, sum_q, sum_k = hand_over(*attention(
        tile_lists[0, 0], q_raw[0], k_raw[0], values[0], grad_out[0],
        gain_q.reshape(heads, HD), gain_k.reshape(heads, HD),
    ))
    return (
        grad_q[None],
        grad_k[None],
        grad_values[None],
        sum_q.reshape(width),
        sum_k.reshape(width),
    )


def solution(mesh):
    rows = P("batch", "tm", "tensor")
    return jax.shard_map(
        shards,
        mesh=mesh,
        in_specs=(rows, rows, rows, rows, P("tensor"), P("tensor"), P("batch", "tm", None)),
        out_specs=(rows, rows, rows, P("tensor"), P("tensor")),
        check_vma=False,
    )
```

```python
import math

import jax
import jax.numpy as jnp
from jax import lax
from jax.experimental import pallas as pl
from jax.experimental.pallas import tpu as pltpu
from jax.sharding import PartitionSpec as P

HD = 128
EPSILON = 1e-06
DEAD = 1e30
SCALE = HD ** (-0.5)
SCALE2 = SCALE * math.log2(math.e)
GROUP = 2
AHEAD = 2
FIRST = 3
PACE = 1
BEGIN = 2
EXTRA = 1
MESH = pl.DeviceIdType.MESH


def cols_dot(left, right):
    return lax.dot_general(
        left, right, (((1,), (1,)), ((), ())), preferred_element_type=jnp.float32
    )


def rows_dot(left, right):
    return lax.dot_general(
        left, right, (((0,), (0,)), ((), ())), preferred_element_type=jnp.float32
    )


def tile_stats(key, value, query, grad):
    scores = cols_dot(key, query) * SCALE2
    highest = jnp.max(scores, axis=0, keepdims=True)
    exponent = jnp.exp2(scores - highest)
    dprobs = cols_dot(value, grad)
    total = jnp.sum(exponent, axis=0, keepdims=True)
    weighted = jnp.sum(exponent * dprobs, axis=0, keepdims=True)
    return highest + jnp.log2(total), weighted / total


def paced(step, chunks):
    return PACE * (step - (chunks - BEGIN)), step - 2


def attention_body(group, chunks, list_hbm, q_hbm, k_hbm, v_hbm, g_hbm, gq_hbm, gk_hbm,
                   gq, gk, dv, sum_q, sum_k,
                   entries, gain_q, gain_k, q_raw, k_raw, v, g, q, k, dq, dk, inv, pull, squares, proj,
                   rq, rg, dq_out, dq_in, st_own, st_out, st_in, co_own, co_out, co_in,
                   pj_own, pj_out, pj_in, pq, terms, term_in, planes,
                   in_sem, sq_send, sq_recv, pk_send, pk_recv, pq_send, pq_recv,
                   tb_send, tb_recv, tz_send, tz_recv, pj_send, pj_recv,
                   bulk_send, bulk_recv, st_send, st_recv, co_send, co_recv, dq_send, dq_recv,
                   relay):
    rows, width = q.shape
    heads = group * chunks
    ahead = min(AHEAD, chunks)
    first = min(FIRST, chunks)
    core = lax.axis_index("tensor")
    cores = lax.axis_size("tensor")
    me = lax.axis_index("tm")
    peers = lax.axis_size("tm")
    clip = lax.axis_index("batch")
    clips = lax.axis_size("batch")
    levels = clips.bit_length() - 1
    assert clips == 1 << levels
    partners = [
        clip + (1 << level) * (1 - 2 * (lax.div(clip, 1 << level) % 2)) for level in range(levels)
    ]
    has = (me > 0, me < peers - 1)
    target = (jnp.maximum(me - 1, 0), jnp.minimum(me + 1, peers - 1))

    def column(head):
        return pl.ds(pl.multiple_of(head * HD, HD), HD)

    def part(chunk):
        return pl.ds(pl.multiple_of(chunk * group * HD, HD), group * HD)

    def members(chunk):
        return pl.ds(chunk * group, group)

    def remote(source, sink, send, recv, **where):
        return pltpu.make_async_remote_copy(
            src_ref=source, dst_ref=sink, send_sem=send, recv_sem=recv,
            device_id=where, device_id_type=MESH,
        )

    def grad_copy(chunk, side, slot):
        cols = part(chunk)
        return remote(g_hbm.at[:, cols], rg.at[slot, :, cols],
                      bulk_send.at[side, 0, chunk], bulk_recv.at[slot, 0, chunk], tm=target[side])

    def query_copy(chunk, side, slot):
        cols = part(chunk)
        return remote(q.at[:, cols], rq.at[slot, :, cols],
                      bulk_send.at[side, 1, chunk], bulk_recv.at[slot, 1, chunk], tm=target[side])

    def stat_copy(chunk, side, slot):
        some = members(chunk)
        return remote(st_out.at[side, some], st_in.at[slot, some],
                      st_send.at[side, chunk], st_recv.at[slot, chunk], tm=target[side])

    def comb_copy(chunk, side, slot):
        some = members(chunk)
        return remote(co_out.at[side, some], co_in.at[slot, some],
                      co_send.at[side, chunk], co_recv.at[slot, chunk], tm=target[side])

    def dq_copy(chunk, side, slot):
        cols = part(chunk)
        return remote(dq_out.at[side, :, cols], dq_in.at[slot, :, cols],
                      dq_send.at[side, chunk], dq_recv.at[slot, chunk], tm=target[side])

    def pj_copy(side, slot):
        return remote(pj_out.at[side], pj_in.at[slot], pj_send.at[side], pj_recv.at[slot],
                      tm=target[side])

    def square_copy(index, slot, peer):
        return remote(squares.at[slot, index], squares.at[slot, index],
                      sq_send.at[index, peer], sq_recv.at[index, slot], tensor=peer)

    def proj_copy(slot, peer):
        return remote(proj.at[slot], proj.at[slot], pk_send.at[peer], pk_recv.at[slot], tensor=peer)

    def pq_copy(slot, peer):
        return remote(pq.at[slot], pq.at[slot], pq_send.at[peer], pq_recv.at[slot], tensor=peer)

    def term_copy(level):
        return remote(terms.at[level], term_in.at[level], tb_send.at[level], tb_recv.at[level],
                      batch=partners[level])

    def plane_copy(slot, peer):
        return remote(planes.at[slot], planes.at[slot], tz_send.at[peer], tz_recv.at[slot], tm=peer)

    def other(mine, count, i):
        return lax.rem(mine + i, count)

    def each_side(do):
        for side in range(2):
            @pl.when(has[side])
            def _():
                do(side)

    loads = [
        pltpu.make_async_copy(source, sink, in_sem.at[i])
        for i, (source, sink) in enumerate((
            (q_hbm, q_raw), (k_hbm, k_raw), (gq_hbm, gain_q), (gk_hbm, gain_k),
            (v_hbm, v), (g_hbm, g), (list_hbm, entries)))
    ]

    barrier = pltpu.get_barrier_semaphore()
    each_side(lambda side: pl.semaphore_signal(
        barrier, inc=1, device_id={"tm": target[side]}, device_id_type=MESH))
    for i in range(1, cores):
        pl.semaphore_signal(
            barrier, inc=1, device_id={"tensor": other(core, cores, i)}, device_id_type=MESH)
    for partner in partners:
        pl.semaphore_signal(barrier, inc=1, device_id={"batch": partner}, device_id_type=MESH)
    for load in loads:
        load.start()
    pl.semaphore_wait(
        barrier, has[0].astype(jnp.int32) + has[1].astype(jnp.int32) + cores - 1 + len(partners))

    for chunk in range(first):
        each_side(lambda side: grad_copy(chunk, side, 1 - side).start())

    block = math.gcd(rows, 128)
    for index, raw in enumerate((q_raw, k_raw)):
        loads[index].wait()
        for top in range(0, rows, block):
            total = jnp.zeros((block, HD), jnp.float32)
            for left in range(0, width, HD):
                wide = raw[top:top + block, left:left + HD].astype(jnp.float32)
                total = total + wide * wide
            squares[core, index, top:top + block, :] = total
        for i in range(1, cores):
            square_copy(index, core, other(core, cores, i)).start()

    for load in loads[2:4]:
        load.wait()
    for index, (raw, gain, out) in enumerate(((q_raw, gain_q, q), (k_raw, gain_k, k))):
        for i in range(1, cores):
            peer = other(core, cores, i)
            square_copy(index, core, peer).wait_send()
            square_copy(index, peer, peer).wait_recv()
        for top in range(0, rows, block):
            total = squares[0, index, top:top + block, :]
            for slot in range(1, cores):
                total = total + squares[slot, index, top:top + block, :]
            mean = jnp.sum(total, axis=1, keepdims=True) / (width * cores)
            inv[index, top:top + block, :] = jnp.broadcast_to(
                lax.rsqrt(mean + EPSILON), (block, HD))

        def norm(head, carry):
            col = column(head)
            out[:, col] = (
                raw[:, col].astype(jnp.float32) * inv[index] * gain[pl.ds(head, 1), :]
            ).astype(out.dtype)
            return carry

        early = 0
        if index == 0:
            early = ahead
            for chunk in range(early):
                lax.fori_loop(chunk * group, (chunk + 1) * group, norm, 0)
                each_side(lambda side: query_copy(chunk, side, 1 - side).start())
        lax.fori_loop(early * group, heads, norm, 0)

    for load in loads[4:]:
        load.wait()
    alive = tuple(
        has[side] & (
            (entries[0] == target[side]) | (entries[1] == target[side])
            | (entries[2] == target[side]))
        for side in range(2)
    )
    for side in range(2):
        @pl.when(jnp.logical_not(has[side]))
        def _():
            for ref in (rq, rg, dq_in, st_in, co_in, pj_in):
                ref[side] = jnp.zeros(ref.shape[1:], ref.dtype)
    pj_own[...] = jnp.zeros(pj_own.shape, jnp.float32)
    pj_out[...] = jnp.zeros(pj_out.shape, jnp.float32)
    proj[core] = jnp.zeros((rows, HD), jnp.float32)

    def put(ref, index, values):
        for row, value in enumerate(values):
            ref[index + (slice(row, row + 1), slice(None))] = value

    def combine(chunk):
        some = members(chunk)
        own = st_own[some, 0:1, :]
        sides = [st_in[side, some, 0:1, :] for side in range(2)]
        highest = own
        for side in range(2):
            highest = jnp.where(alive[side], jnp.maximum(highest, sides[side]), highest)
        weight = jnp.exp2(own - highest)
        total = weight
        delta = weight * st_own[some, 1:2, :]
        for side in range(2):
            weight = jnp.where(
                alive[side], jnp.exp2(jnp.minimum(sides[side] - highest, 0.0)), 0.0)
            total = total + weight
            delta = delta + jnp.where(alive[side], weight * st_in[side, some, 1:2, :], 0.0)
        whole = highest + jnp.log2(total)
        delta = delta / total
        co_own[some, 0:1, :] = whole
        co_own[some, 1:2, :] = delta
        for side in range(2):
            co_out[side, some, 0:1, :] = jnp.where(alive[side], whole, DEAD)
            co_out[side, some, 1:2, :] = delta

    def backward(head):
        col = column(head)
        key = k[:, col]
        value = v[:, col]
        key_total = None
        value_total = None
        for t in range(3):
            if t < 2:
                query, grad, stat = rq[t, :, col], rg[t, :, col], co_in.at[t]
            else:
                query, grad, stat = q[:, col], g[:, col], co_own
            scores = cols_dot(key, query) * SCALE2
            probs = jnp.exp2(scores - stat[head, 0:1, :])
            dprobs = cols_dot(value, grad)
            wide = probs * (dprobs - stat[head, 1:2, :])
            pulled = jnp.sum(wide * scores, axis=0, keepdims=True)
            dscore = wide.astype(jnp.bfloat16)
            probs_b = probs.astype(jnp.bfloat16)
            value_term = jnp.dot(probs_b, grad, preferred_element_type=jnp.float32)
            key_term = jnp.dot(dscore, query, preferred_element_type=jnp.float32)
            value_total = value_term if t == 0 else value_total + value_term
            key_total = key_term if t == 0 else key_total + key_term
            result = rows_dot(key, dscore).T * SCALE
            if t < 2:
                dq_out[t, :, col] = result.astype(dq_out.dtype)
                pj_out[t] = pj_out[t] + pulled
            else:
                dq[:, col] = result
                pj_own[...] = pj_own[...] + pulled
        key_total = key_total * SCALE
        dk[:, col] = key_total
        both = k_raw[:, col].astype(jnp.float32) * key_total
        terms[0, pl.ds(head, 1), :] = jnp.sum(both * inv[1], axis=0, keepdims=True)
        proj[core] = proj[core] + both * gain_k[pl.ds(head, 1), :]
        dv[:, col] = value_total.astype(dv.dtype)

    def start_dq(chunk, carry):
        each_side(lambda side: dq_copy(chunk, side, 1 - side).start())
        return carry

    def settle(chunk):
        def done(side):
            grad_copy(chunk, side, 1 - side).wait_send()
            query_copy(chunk, side, 1 - side).wait_send()
            stat_copy(chunk, side, 1 - side).wait_send()
            comb_copy(chunk, side, 1 - side).wait_send()

        each_side(done)

    rounds = peers - 2
    steps = chunks + 2

    def relay_signal():
        each_side(lambda side: pl.semaphore_signal(
            relay.at[1 - side], inc=1, device_id={"tm": target[side]}, device_id_type=MESH))

    def relay_wait():
        each_side(lambda side: pl.semaphore_wait(relay.at[side], 1))

    def sent(s):
        wish, done = paced(s, chunks)
        return jnp.clip(jnp.minimum(wish, done), 0, chunks)

    def step(s, carry):
        @pl.when((s >= 1) & (s <= rounds))
        def _():
            relay_wait()

        @pl.when(s < rounds)
        def _():
            relay_signal()

        @pl.when(s < chunks)
        def _():
            def arrive(side):
                grad_copy(s, side, side).wait_recv()
                query_copy(s, side, side).wait_recv()

            each_side(arrive)
            for inner in range(group):
                head = s * group + inner
                col = column(head)
                for side in range(2):
                    put(st_out, (side, head), tile_stats(
                        k[:, col], v[:, col], rq[side, :, col], rg[side, :, col]))
            each_side(lambda side: stat_copy(s, side, 1 - side).start())

        @pl.when((s >= 1) & (s <= chunks))
        def _():
            each_side(lambda side: stat_copy(s - 1, side, side).wait_recv())
            combine(s - 1)
            each_side(lambda side: comb_copy(s - 1, side, 1 - side).start())

        @pl.when(s + ahead < chunks)
        def _():
            each_side(lambda side: query_copy(s + ahead, side, 1 - side).start())

        @pl.when(s + first < chunks)
        def _():
            each_side(lambda side: grad_copy(s + first, side, 1 - side).start())

        lax.fori_loop(sent(s), sent(s + 1), start_dq, 0)

        @pl.when(s < chunks)
        def _():
            for inner in range(group):
                head = s * group + inner
                col = column(head)
                put(st_own, (head,), tile_stats(k[:, col], v[:, col], q[:, col], g[:, col]))

        @pl.when(s >= 2)
        def _():
            each_side(lambda side: comb_copy(s - 2, side, side).wait_recv())
            for inner in range(group):
                backward((s - 2) * group + inner)

        @pl.when(s >= 3)
        def _():
            settle(s - 3)

        return carry

    lax.fori_loop(0, steps, step, 0)

    each_side(lambda side: pj_copy(side, 1 - side).start())
    if levels:
        term_copy(0).start()
    for i in range(1, cores):
        proj_copy(core, other(core, cores, i)).start()
    begun = min(max(min(*paced(steps, chunks)), 0), chunks)
    early = min(begun + EXTRA, chunks)
    lax.fori_loop(begun, early, start_dq, 0)

    if rounds >= steps:
        relay_wait()
        for _ in range(steps, rounds):
            relay_signal()
            relay_wait()

    def pull_of(index, projection):
        inverse = inv[index]
        pull[index] = inverse * inverse * projection / (width * cores)

    def finish(index, raw, gain, normed, out, head):
        col = column(head)
        out[:, col] = (
            inv[index] * gain[pl.ds(head, 1), :] * normed
            - raw[:, col].astype(jnp.float32) * pull[index]
        ).astype(out.dtype)

    for i in range(1, cores):
        peer = other(core, cores, i)
        proj_copy(core, peer).wait_send()
        proj_copy(peer, peer).wait_recv()
    total = proj[0]
    for slot in range(1, cores):
        total = total + proj[slot]
    pull_of(1, inv[1] * jnp.sum(total, axis=1, keepdims=True))

    each_side(lambda side: pj_copy(side, side).wait_recv())
    pq[core] = pj_own[...] + pj_in[0] + pj_in[1]
    for i in range(1, cores):
        pq_copy(core, other(core, cores, i)).start()

    for level in range(levels):
        term_copy(level).wait_send()
        term_copy(level).wait_recv()
        terms[level + 1] = terms[level] + term_in[level]
        if level + 1 < levels:
            term_copy(level + 1).start()
    planes[me] = terms[levels]
    for i in range(1, peers):
        plane_copy(me, other(me, peers, i)).start()
    lax.fori_loop(early, chunks, start_dq, 0)

    def keys(head, carry):
        finish(1, k_raw, gain_k, dk[:, column(head)], gk, head)
        return carry

    lax.fori_loop(0, heads, keys, 0)

    for i in range(1, cores):
        peer = other(core, cores, i)
        pq_copy(core, peer).wait_send()
        pq_copy(peer, peer).wait_recv()
    row = pq[0]
    for slot in range(1, cores):
        row = row + pq[slot]
    pull_of(0, jnp.broadcast_to(row * (SCALE / SCALE2), (HD, rows)).T)

    settle(chunks - 1)
    each_side(lambda side: pj_copy(side, 1 - side).wait_send())

    def queries(chunk, carry):
        @pl.when(chunk == chunks - 1)
        def _():
            for i in range(1, peers):
                peer = other(me, peers, i)
                plane_copy(me, peer).wait_send()
                plane_copy(peer, peer).wait_recv()
            whole = jnp.sum(planes[...], axis=0) * (1.0 / math.sqrt(clips * peers * rows))
            sum_k[...] = whole
            sum_q[...] = whole * gain_k[...] / gain_q[...]

        @pl.when(chunk >= 1)
        def _():
            each_side(lambda side: dq_copy(chunk - 1, side, 1 - side).wait_send())

        each_side(lambda side: dq_copy(chunk, side, side).wait_recv())
        for inner in range(group):
            head = chunk * group + inner
            col = column(head)
            normed = (
                dq[:, col]
                + dq_in[0, :, col].astype(jnp.float32)
                + dq_in[1, :, col].astype(jnp.float32)
            )
            finish(0, q_raw, gain_q, normed, gq, head)
        return carry

    lax.fori_loop(0, chunks, queries, 0)

    each_side(lambda side: dq_copy(chunks - 1, side, 1 - side).wait_send())


def attention(entries, query, key, value, grad, gain_q, gain_k):
    rows, width = query.shape
    heads = width // HD
    group = math.gcd(GROUP, heads)
    chunks = heads // group
    cores = lax.axis_size("tensor")
    peers = lax.axis_size("tm")
    clips = lax.axis_size("batch")
    vmem = pl.BlockSpec(memory_space=pltpu.VMEM)
    hbm = pl.BlockSpec(memory_space=pltpu.HBM)
    dma = pltpu.SemaphoreType.DMA
    full = jax.ShapeDtypeStruct((rows, width), jnp.bfloat16)
    gain = jax.ShapeDtypeStruct((heads, HD), jnp.float32)

    def f32(*shape):
        return pltpu.VMEM(shape, jnp.float32)

    def bf16(*shape):
        return pltpu.VMEM(shape, jnp.bfloat16)

    def body(*refs):
        attention_body(group, chunks, *refs)

    pinned = [
        pltpu.with_memory_space_constraint(x, pltpu.HBM)
        for x in (entries, query, key, value, grad, gain_q, gain_k)
    ]
    return pl.pallas_call(
        body,
        out_shape=[full, full, full, gain, gain],
        in_specs=[hbm] * 7,
        out_specs=[vmem] * 5,
        scratch_shapes=(
            [pltpu.SMEM(entries.shape, jnp.int32)] + [f32(heads, HD)] * 2
            + [bf16(rows, width)] * 6 + [f32(rows, width)] * 2
            + [f32(2, rows, HD)] * 2 + [f32(cores, 2, rows, HD), f32(cores, rows, HD)]
            + [bf16(2, rows, width)] * 4
            + [f32(heads, 2, rows), f32(2, heads, 2, rows), f32(2, heads, 2, rows)] * 2
            + [f32(1, rows), f32(2, 1, rows), f32(2, 1, rows), f32(cores, 1, rows)]
            + [f32(clips.bit_length(), heads, HD)] * 2 + [f32(peers, heads, HD)]
            + [dma((7,)), dma((2, cores)), dma((2, cores))]
            + [dma((cores,))] * 4 + [dma((clips.bit_length(),))] * 2 + [dma((peers,))] * 2 + [dma((2,))] * 2
            + [dma((2, 2, chunks))] * 2 + [dma((2, chunks))] * 6
            + [pltpu.SemaphoreType.REGULAR((2,))]
        ),
        compiler_params=pltpu.CompilerParams(
            collective_id=0, has_side_effects=True, vmem_limit_bytes=36 << 20),
        name="attention",
    )(*pinned)


def hand_over(*arrays):
    count = len(arrays)
    hbm = pl.BlockSpec(memory_space=pltpu.HBM)

    def body(*refs):
        sems = refs[2 * count]
        copies = [
            pltpu.make_async_copy(refs[i], refs[count + i], sems.at[i]) for i in range(count)
        ]
        for copy in copies:
            copy.start()
        for copy in copies:
            copy.wait()

    return pl.pallas_call(
        body,
        out_shape=[jax.ShapeDtypeStruct(x.shape, x.dtype) for x in arrays],
        in_specs=[pl.BlockSpec(memory_space=pl.ANY)] * count,
        out_specs=[hbm] * count,
        scratch_shapes=[pltpu.SemaphoreType.DMA((count,))],
        compiler_params=pltpu.CompilerParams(vmem_limit_bytes=1 << 20),
        name="hand_over",
    )(*arrays)


def shards(q_raw, k_raw, values, grad_out, gain_q, gain_k, tile_lists):
    width = q_raw.shape[2]
    heads = width // HD
    grad_q, grad_k, grad_values, sum_q, sum_k = hand_over(*attention(
        tile_lists[0, 0], q_raw[0], k_raw[0], values[0], grad_out[0],
        gain_q.reshape(heads, HD), gain_k.reshape(heads, HD),
    ))
    return (
        grad_q[None],
        grad_k[None],
        grad_values[None],
        sum_q.reshape(width),
        sum_k.reshape(width),
    )


def solution(mesh):
    rows = P("batch", "tm", "tensor")
    return jax.shard_map(
        shards,
        mesh=mesh,
        in_specs=(rows, rows, rows, rows, P("tensor"), P("tensor"), P("batch", "tm", None)),
        out_specs=(rows, rows, rows, P("tensor"), P("tensor")),
        check_vma=False,
    )
```

```python
import math

import jax
import jax.numpy as jnp
from jax import lax
from jax.experimental import pallas as pl
from jax.experimental.pallas import tpu as pltpu
from jax.sharding import PartitionSpec as P

HD = 128
EPSILON = 1e-06
DEAD = 1e30
SCALE = HD ** (-0.5)
SCALE2 = SCALE * math.log2(math.e)
GROUP = 2
AHEAD = 2
FIRST = 3
PACE = 1
BEGIN = 2
EXTRA = 1
MESH = pl.DeviceIdType.MESH


def cols_dot(left, right):
    return lax.dot_general(
        left, right, (((1,), (1,)), ((), ())), preferred_element_type=jnp.float32
    )


def rows_dot(left, right):
    return lax.dot_general(
        left, right, (((0,), (0,)), ((), ())), preferred_element_type=jnp.float32
    )


def tile_stats(key, value, query, grad):
    scores = cols_dot(key, query) * SCALE2
    highest = jnp.max(scores, axis=0, keepdims=True)
    exponent = jnp.exp2(scores - highest)
    dprobs = cols_dot(value, grad)
    total = jnp.sum(exponent, axis=0, keepdims=True)
    weighted = jnp.sum(exponent * dprobs, axis=0, keepdims=True)
    return highest + jnp.log2(total), weighted / total


def paced(step, chunks):
    return PACE * (step - (chunks - BEGIN)), step - 2


def attention_body(group, chunks, list_hbm, q_hbm, k_hbm, v_hbm, g_hbm, gq_hbm, gk_hbm,
                   gq, gk, dv, sum_q, sum_k,
                   entries, gain_q, gain_k, q_raw, k_raw, v, g, q, k, dq, dk, inv, pull, squares, proj,
                   rq, rg, dq_out, dq_in, st_own, st_out, st_in, co_own, co_out, co_in,
                   pj_own, pj_out, pj_in, pq, terms, term_in, planes,
                   in_sem, sq_send, sq_recv, pk_send, pk_recv, pq_send, pq_recv,
                   tb_send, tb_recv, tz_send, tz_recv, pj_send, pj_recv,
                   bulk_send, bulk_recv, st_send, st_recv, co_send, co_recv, dq_send, dq_recv,
                   relay, tm_open, core_open, clip_open):
    rows, width = q.shape
    heads = group * chunks
    ahead = min(AHEAD, chunks)
    first = min(FIRST, chunks)
    core = lax.axis_index("tensor")
    cores = lax.axis_size("tensor")
    me = lax.axis_index("tm")
    peers = lax.axis_size("tm")
    clip = lax.axis_index("batch")
    clips = lax.axis_size("batch")
    levels = clips.bit_length() - 1
    assert clips == 1 << levels
    bits = [lax.rem(lax.div(clip, 1 << level), 2) for level in range(levels)]
    partners = [clip + (1 << level) * (1 - 2 * bits[level]) for level in range(levels)]
    has = (me > 0, me < peers - 1)
    target = (jnp.maximum(me - 1, 0), jnp.minimum(me + 1, peers - 1))

    def column(head):
        return pl.ds(pl.multiple_of(head * HD, HD), HD)

    def part(chunk):
        return pl.ds(pl.multiple_of(chunk * group * HD, HD), group * HD)

    def members(chunk):
        return pl.ds(chunk * group, group)

    def remote(source, sink, send, recv, **where):
        return pltpu.make_async_remote_copy(
            src_ref=source, dst_ref=sink, send_sem=send, recv_sem=recv,
            device_id=where, device_id_type=MESH,
        )

    def grad_copy(chunk, side, slot):
        cols = part(chunk)
        return remote(g_hbm.at[:, cols], rg.at[slot, :, cols],
                      bulk_send.at[side, 0, chunk], bulk_recv.at[slot, 0, chunk], tm=target[side])

    def query_copy(chunk, side, slot):
        cols = part(chunk)
        return remote(q.at[:, cols], rq.at[slot, :, cols],
                      bulk_send.at[side, 1, chunk], bulk_recv.at[slot, 1, chunk], tm=target[side])

    def stat_copy(chunk, side, slot):
        some = members(chunk)
        return remote(st_out.at[side, some], st_in.at[slot, some],
                      st_send.at[side, chunk], st_recv.at[slot, chunk], tm=target[side])

    def comb_copy(chunk, side, slot):
        some = members(chunk)
        return remote(co_out.at[side, some], co_in.at[slot, some],
                      co_send.at[side, chunk], co_recv.at[slot, chunk], tm=target[side])

    def dq_copy(chunk, side, slot):
        cols = part(chunk)
        return remote(dq_out.at[side, :, cols], dq_in.at[slot, :, cols],
                      dq_send.at[side, chunk], dq_recv.at[slot, chunk], tm=target[side])

    def pj_copy(side, slot):
        return remote(pj_out.at[side], pj_in.at[slot], pj_send.at[side], pj_recv.at[slot],
                      tm=target[side])

    def square_copy(index, slot, peer):
        return remote(squares.at[slot, index], squares.at[slot, index],
                      sq_send.at[index, peer], sq_recv.at[index, slot], tensor=peer)

    def proj_copy(slot, peer):
        return remote(proj.at[slot], proj.at[slot], pk_send.at[peer], pk_recv.at[slot], tensor=peer)

    def pq_copy(slot, peer):
        return remote(pq.at[slot], pq.at[slot], pq_send.at[peer], pq_recv.at[slot], tensor=peer)

    def term_copy(level):
        return remote(terms.at[level], term_in.at[level], tb_send.at[level], tb_recv.at[level],
                      batch=partners[level])

    def plane_copy(slot, peer):
        return remote(planes.at[slot], planes.at[slot], tz_send.at[peer], tz_recv.at[slot], tm=peer)

    def other(mine, count, i):
        return lax.rem(mine + i, count)

    def each_side(do):
        for side in range(2):
            @pl.when(has[side])
            def _():
                do(side)

    loads = [
        pltpu.make_async_copy(source, sink, in_sem.at[i])
        for i, (source, sink) in enumerate((
            (q_hbm, q_raw), (k_hbm, k_raw), (gq_hbm, gain_q), (gk_hbm, gain_k),
            (v_hbm, v), (g_hbm, g), (list_hbm, entries)))
    ]

    barrier = pltpu.get_barrier_semaphore()

    def tell(semaphore, **where):
        pl.semaphore_signal(semaphore, inc=1, device_id=where, device_id_type=MESH)

    @pl.when(has[1])
    def _():
        tell(barrier, tm=target[1])

    for i in range(1, cores):
        @pl.when(core + i < cores)
        def _():
            tell(barrier, tensor=jnp.minimum(core + i, cores - 1))

    for level in range(levels):
        @pl.when(bits[level] == 0)
        def _():
            tell(barrier, batch=partners[level])

    for load in loads:
        load.start()
    below = has[0].astype(jnp.int32) + core + sum(bits)

    @pl.when(below > 0)
    def _():
        pl.semaphore_wait(barrier, below)

    @pl.when(has[0])
    def _():
        tell(tm_open, tm=target[0])
        for chunk in range(first):
            grad_copy(chunk, 0, 1).start()

    for i in range(1, cores):
        @pl.when(core >= i)
        def _():
            tell(core_open, tensor=jnp.maximum(core - i, 0))

    for level in range(levels):
        @pl.when(bits[level] == 1)
        def _():
            tell(clip_open.at[level], batch=partners[level])

    @pl.when(has[1])
    def _():
        pl.semaphore_wait(tm_open, 1)
        for chunk in range(first):
            grad_copy(chunk, 1, 0).start()

    def open_level(level):
        @pl.when(bits[level] == 0)
        def _():
            pl.semaphore_wait(clip_open.at[level], 1)

    block = math.gcd(rows, 128)
    for index, raw in enumerate((q_raw, k_raw)):
        loads[index].wait()
        for top in range(0, rows, block):
            total = jnp.zeros((block, HD), jnp.float32)
            for left in range(0, width, HD):
                wide = raw[top:top + block, left:left + HD].astype(jnp.float32)
                total = total + wide * wide
            squares[core, index, top:top + block, :] = total
        if index == 0:
            @pl.when(core < cores - 1)
            def _():
                pl.semaphore_wait(core_open, cores - 1 - core)

        for i in range(1, cores):
            square_copy(index, core, other(core, cores, i)).start()

    for load in loads[2:4]:
        load.wait()
    for index, (raw, gain, out) in enumerate(((q_raw, gain_q, q), (k_raw, gain_k, k))):
        for i in range(1, cores):
            peer = other(core, cores, i)
            square_copy(index, core, peer).wait_send()
            square_copy(index, peer, peer).wait_recv()
        for top in range(0, rows, block):
            total = squares[0, index, top:top + block, :]
            for slot in range(1, cores):
                total = total + squares[slot, index, top:top + block, :]
            mean = jnp.sum(total, axis=1, keepdims=True) / (width * cores)
            inv[index, top:top + block, :] = jnp.broadcast_to(
                lax.rsqrt(mean + EPSILON), (block, HD))

        def norm(head, carry):
            col = column(head)
            out[:, col] = (
                raw[:, col].astype(jnp.float32) * inv[index] * gain[pl.ds(head, 1), :]
            ).astype(out.dtype)
            return carry

        early = 0
        if index == 0:
            early = ahead
            for chunk in range(early):
                lax.fori_loop(chunk * group, (chunk + 1) * group, norm, 0)
                each_side(lambda side: query_copy(chunk, side, 1 - side).start())
        lax.fori_loop(early * group, heads, norm, 0)

    for load in loads[4:]:
        load.wait()
    alive = tuple(
        has[side] & (
            (entries[0] == target[side]) | (entries[1] == target[side])
            | (entries[2] == target[side]))
        for side in range(2)
    )
    for side in range(2):
        @pl.when(jnp.logical_not(has[side]))
        def _():
            for ref in (rq, rg, dq_in, st_in, co_in, pj_in):
                ref[side] = jnp.zeros(ref.shape[1:], ref.dtype)
    pj_own[...] = jnp.zeros(pj_own.shape, jnp.float32)
    pj_out[...] = jnp.zeros(pj_out.shape, jnp.float32)
    proj[core] = jnp.zeros((rows, HD), jnp.float32)

    def put(ref, index, values):
        for row, value in enumerate(values):
            ref[index + (slice(row, row + 1), slice(None))] = value

    def combine(chunk):
        some = members(chunk)
        own = st_own[some, 0:1, :]
        sides = [st_in[side, some, 0:1, :] for side in range(2)]
        highest = own
        for side in range(2):
            highest = jnp.where(alive[side], jnp.maximum(highest, sides[side]), highest)
        weight = jnp.exp2(own - highest)
        total = weight
        delta = weight * st_own[some, 1:2, :]
        for side in range(2):
            weight = jnp.where(
                alive[side], jnp.exp2(jnp.minimum(sides[side] - highest, 0.0)), 0.0)
            total = total + weight
            delta = delta + jnp.where(alive[side], weight * st_in[side, some, 1:2, :], 0.0)
        whole = highest + jnp.log2(total)
        delta = delta / total
        co_own[some, 0:1, :] = whole
        co_own[some, 1:2, :] = delta
        for side in range(2):
            co_out[side, some, 0:1, :] = jnp.where(alive[side], whole, DEAD)
            co_out[side, some, 1:2, :] = delta

    def backward(head):
        col = column(head)
        key = k[:, col]
        value = v[:, col]
        key_total = None
        value_total = None
        for t in range(3):
            if t < 2:
                query, grad, stat = rq[t, :, col], rg[t, :, col], co_in.at[t]
            else:
                query, grad, stat = q[:, col], g[:, col], co_own
            scores = cols_dot(key, query) * SCALE2
            probs = jnp.exp2(scores - stat[head, 0:1, :])
            dprobs = cols_dot(value, grad)
            wide = probs * (dprobs - stat[head, 1:2, :])
            pulled = jnp.sum(wide * scores, axis=0, keepdims=True)
            dscore = wide.astype(jnp.bfloat16)
            probs_b = probs.astype(jnp.bfloat16)
            value_term = jnp.dot(probs_b, grad, preferred_element_type=jnp.float32)
            key_term = jnp.dot(dscore, query, preferred_element_type=jnp.float32)
            value_total = value_term if t == 0 else value_total + value_term
            key_total = key_term if t == 0 else key_total + key_term
            result = rows_dot(key, dscore).T * SCALE
            if t < 2:
                dq_out[t, :, col] = result.astype(dq_out.dtype)
                pj_out[t] = pj_out[t] + pulled
            else:
                dq[:, col] = result
                pj_own[...] = pj_own[...] + pulled
        key_total = key_total * SCALE
        dk[:, col] = key_total
        both = k_raw[:, col].astype(jnp.float32) * key_total
        terms[0, pl.ds(head, 1), :] = jnp.sum(both * inv[1], axis=0, keepdims=True)
        proj[core] = proj[core] + both * gain_k[pl.ds(head, 1), :]
        dv[:, col] = value_total.astype(dv.dtype)

    def start_dq(chunk, carry):
        each_side(lambda side: dq_copy(chunk, side, 1 - side).start())
        return carry

    def settle(chunk):
        def done(side):
            grad_copy(chunk, side, 1 - side).wait_send()
            query_copy(chunk, side, 1 - side).wait_send()
            stat_copy(chunk, side, 1 - side).wait_send()
            comb_copy(chunk, side, 1 - side).wait_send()

        each_side(done)

    rounds = peers - 2
    steps = chunks + 2

    def relay_signal():
        each_side(lambda side: pl.semaphore_signal(
            relay.at[1 - side], inc=1, device_id={"tm": target[side]}, device_id_type=MESH))

    def relay_wait():
        each_side(lambda side: pl.semaphore_wait(relay.at[side], 1))

    def sent(s):
        wish, done = paced(s, chunks)
        return jnp.clip(jnp.minimum(wish, done), 0, chunks)

    def step(s, carry):
        @pl.when((s >= 1) & (s <= rounds))
        def _():
            relay_wait()

        @pl.when(s < rounds)
        def _():
            relay_signal()

        @pl.when(s < chunks)
        def _():
            def arrive(side):
                grad_copy(s, side, side).wait_recv()
                query_copy(s, side, side).wait_recv()

            each_side(arrive)
            for inner in range(group):
                head = s * group + inner
                col = column(head)
                for side in range(2):
                    put(st_out, (side, head), tile_stats(
                        k[:, col], v[:, col], rq[side, :, col], rg[side, :, col]))
            each_side(lambda side: stat_copy(s, side, 1 - side).start())

        @pl.when((s >= 1) & (s <= chunks))
        def _():
            each_side(lambda side: stat_copy(s - 1, side, side).wait_recv())
            combine(s - 1)
            each_side(lambda side: comb_copy(s - 1, side, 1 - side).start())

        @pl.when(s + ahead < chunks)
        def _():
            each_side(lambda side: query_copy(s + ahead, side, 1 - side).start())

        @pl.when(s + first < chunks)
        def _():
            each_side(lambda side: grad_copy(s + first, side, 1 - side).start())

        lax.fori_loop(sent(s), sent(s + 1), start_dq, 0)

        @pl.when(s < chunks)
        def _():
            for inner in range(group):
                head = s * group + inner
                col = column(head)
                put(st_own, (head,), tile_stats(k[:, col], v[:, col], q[:, col], g[:, col]))

        @pl.when(s >= 2)
        def _():
            each_side(lambda side: comb_copy(s - 2, side, side).wait_recv())
            for inner in range(group):
                backward((s - 2) * group + inner)

        @pl.when(s >= 3)
        def _():
            settle(s - 3)

        return carry

    lax.fori_loop(0, steps, step, 0)

    each_side(lambda side: pj_copy(side, 1 - side).start())
    if levels:
        open_level(0)
        term_copy(0).start()
    for i in range(1, cores):
        proj_copy(core, other(core, cores, i)).start()
    begun = min(max(min(*paced(steps, chunks)), 0), chunks)
    early = min(begun + EXTRA, chunks)
    lax.fori_loop(begun, early, start_dq, 0)

    if rounds >= steps:
        relay_wait()
        for _ in range(steps, rounds):
            relay_signal()
            relay_wait()

    def pull_of(index, projection):
        inverse = inv[index]
        pull[index] = inverse * inverse * projection / (width * cores)

    def finish(index, raw, gain, normed, out, head):
        col = column(head)
        out[:, col] = (
            inv[index] * gain[pl.ds(head, 1), :] * normed
            - raw[:, col].astype(jnp.float32) * pull[index]
        ).astype(out.dtype)

    for level in range(levels):
        term_copy(level).wait_send()
        term_copy(level).wait_recv()
        terms[level + 1] = terms[level] + term_in[level]
        if level + 1 < levels:
            open_level(level + 1)
            term_copy(level + 1).start()
    planes[me] = jnp.pad(terms[levels], ((0, planes.shape[1] - heads), (0, 0))).astype(planes.dtype)
    for i in range(1, peers):
        plane_copy(me, other(me, peers, i)).start()
    lax.fori_loop(early, chunks, start_dq, 0)

    for i in range(1, cores):
        peer = other(core, cores, i)
        proj_copy(core, peer).wait_send()
        proj_copy(peer, peer).wait_recv()
    total = proj[0]
    for slot in range(1, cores):
        total = total + proj[slot]
    pull_of(1, inv[1] * jnp.sum(total, axis=1, keepdims=True))

    each_side(lambda side: pj_copy(side, side).wait_recv())
    pq[core] = pj_own[...] + pj_in[0] + pj_in[1]
    for i in range(1, cores):
        pq_copy(core, other(core, cores, i)).start()

    def keys(head, carry):
        finish(1, k_raw, gain_k, dk[:, column(head)], gk, head)
        return carry

    lax.fori_loop(0, heads, keys, 0)

    for i in range(1, cores):
        peer = other(core, cores, i)
        pq_copy(core, peer).wait_send()
        pq_copy(peer, peer).wait_recv()
    row = pq[0]
    for slot in range(1, cores):
        row = row + pq[slot]
    pull_of(0, jnp.broadcast_to(row * (SCALE / SCALE2), (HD, rows)).T)

    settle(chunks - 1)
    each_side(lambda side: pj_copy(side, 1 - side).wait_send())

    def queries(chunk, carry):
        @pl.when(chunk == chunks - 1)
        def _():
            for i in range(1, peers):
                peer = other(me, peers, i)
                plane_copy(me, peer).wait_send()
                plane_copy(peer, peer).wait_recv()
            whole = jnp.sum(planes[...].astype(jnp.float32), axis=0)[:heads] * (1.0 / math.sqrt(clips * peers * rows))
            sum_k[...] = whole
            sum_q[...] = whole * gain_k[...] / gain_q[...]

        @pl.when(chunk >= 1)
        def _():
            each_side(lambda side: dq_copy(chunk - 1, side, 1 - side).wait_send())

        each_side(lambda side: dq_copy(chunk, side, side).wait_recv())
        for inner in range(group):
            head = chunk * group + inner
            col = column(head)
            normed = (
                dq[:, col]
                + dq_in[0, :, col].astype(jnp.float32)
                + dq_in[1, :, col].astype(jnp.float32)
            )
            finish(0, q_raw, gain_q, normed, gq, head)
        return carry

    lax.fori_loop(0, chunks, queries, 0)

    each_side(lambda side: dq_copy(chunks - 1, side, 1 - side).wait_send())


def attention(entries, query, key, value, grad, gain_q, gain_k):
    rows, width = query.shape
    heads = width // HD
    group = math.gcd(GROUP, heads)
    chunks = heads // group
    cores = lax.axis_size("tensor")
    peers = lax.axis_size("tm")
    clips = lax.axis_size("batch")
    vmem = pl.BlockSpec(memory_space=pltpu.VMEM)
    hbm = pl.BlockSpec(memory_space=pltpu.HBM)
    dma = pltpu.SemaphoreType.DMA
    regular = pltpu.SemaphoreType.REGULAR
    full = jax.ShapeDtypeStruct((rows, width), jnp.bfloat16)
    gain = jax.ShapeDtypeStruct((heads, HD), jnp.float32)

    def f32(*shape):
        return pltpu.VMEM(shape, jnp.float32)

    def bf16(*shape):
        return pltpu.VMEM(shape, jnp.bfloat16)

    def body(*refs):
        attention_body(group, chunks, *refs)

    pinned = [
        pltpu.with_memory_space_constraint(x, pltpu.HBM)
        for x in (entries, query, key, value, grad, gain_q, gain_k)
    ]
    return pl.pallas_call(
        body,
        out_shape=[full, full, full, gain, gain],
        in_specs=[hbm] * 7,
        out_specs=[vmem] * 5,
        scratch_shapes=(
            [pltpu.SMEM(entries.shape, jnp.int32)] + [f32(heads, HD)] * 2
            + [bf16(rows, width)] * 6 + [f32(rows, width)] * 2
            + [f32(2, rows, HD)] * 2 + [f32(cores, 2, rows, HD), f32(cores, rows, HD)]
            + [bf16(2, rows, width)] * 4
            + [f32(heads, 2, rows), f32(2, heads, 2, rows), f32(2, heads, 2, rows)] * 2
            + [f32(1, rows), f32(2, 1, rows), f32(2, 1, rows), f32(cores, 1, rows)]
            + [f32(clips.bit_length(), heads, HD)] * 2 + [bf16(peers, -(-heads // 16) * 16, HD)]
            + [dma((7,)), dma((2, cores)), dma((2, cores))]
            + [dma((cores,))] * 4 + [dma((clips.bit_length(),))] * 2 + [dma((peers,))] * 2 + [dma((2,))] * 2
            + [dma((2, 2, chunks))] * 2 + [dma((2, chunks))] * 6
            + [regular((2,)), regular, regular, regular((clips.bit_length(),))]
        ),
        compiler_params=pltpu.CompilerParams(
            collective_id=0, has_side_effects=True, vmem_limit_bytes=36 << 20),
        name="attention",
    )(*pinned)


def hand_over(*arrays):
    count = len(arrays)
    hbm = pl.BlockSpec(memory_space=pltpu.HBM)

    def body(*refs):
        sems = refs[2 * count]
        copies = [
            pltpu.make_async_copy(refs[i], refs[count + i], sems.at[i]) for i in range(count)
        ]
        for copy in copies:
            copy.start()
        for copy in copies:
            copy.wait()

    return pl.pallas_call(
        body,
        out_shape=[jax.ShapeDtypeStruct(x.shape, x.dtype) for x in arrays],
        in_specs=[pl.BlockSpec(memory_space=pl.ANY)] * count,
        out_specs=[hbm] * count,
        scratch_shapes=[pltpu.SemaphoreType.DMA((count,))],
        compiler_params=pltpu.CompilerParams(vmem_limit_bytes=1 << 20),
        name="hand_over",
    )(*arrays)


def shards(q_raw, k_raw, values, grad_out, gain_q, gain_k, tile_lists):
    width = q_raw.shape[2]
    heads = width // HD
    grad_q, grad_k, grad_values, sum_q, sum_k = hand_over(*attention(
        tile_lists[0, 0], q_raw[0], k_raw[0], values[0], grad_out[0],
        gain_q.reshape(heads, HD), gain_k.reshape(heads, HD),
    ))
    return (
        grad_q[None],
        grad_k[None],
        grad_values[None],
        sum_q.reshape(width),
        sum_k.reshape(width),
    )


def solution(mesh):
    rows = P("batch", "tm", "tensor")
    return jax.shard_map(
        shards,
        mesh=mesh,
        in_specs=(rows, rows, rows, rows, P("tensor"), P("tensor"), P("batch", "tm", None)),
        out_specs=(rows, rows, rows, P("tensor"), P("tensor")),
        check_vma=False,
    )
```
